512 devices in a mesh: seq: 32 (over y, z_lo), head: 16 (over x, z_hi, core).
Axes of the slice: x: 4, y: 4, z: 16 (z_hi: 2, z_lo: 8; z = z_hi * 8 + z_lo), core: 2. Of those that a mesh axis runs over, the one named last changes fastest.
Arguments:
- queries: bfloat16 [16384, 2048], P('seq', 'head'), may hold values from -4.5 to 4.5
- keys: bfloat16 [16384, 2048], P('seq', 'head'), may hold values from -4.5 to 4.5
- values: bfloat16 [16384, 2048], P('seq', 'head'), may hold values from -6 to 6
- grad_out: bfloat16 [16384, 2048], P('seq', 'head'), may hold values from -6 to 6
- block_perm: int32 [16, 32], P('head'), may hold values from 0 to 31, as said below
Outputs:
- attended: bfloat16 [16384, 2048], P('seq', 'head')
- grad_queries: bfloat16 [16384, 2048], P('seq', 'head')
- grad_keys: bfloat16 [16384, 2048], P('seq', 'head')
- grad_values: bfloat16 [16384, 2048], P('seq', 'head')
The draws below stay inside these ranges and needn't reach their ends.
Inputs may be any that keep to these rules, and one draw needn't show every extreme that they name: Each row of block_perm is a permutation of 0 to 31.
All inputs are finite; a program needn't handle non-finite values.
Results may differ from the reference program's by a relative error of at most 0.007.
Values may be sent and summed in bfloat16 or wider, within the bound.
A program may use at most 64 MiB of HBM per device.

```python
import jax
import jax.numpy as jnp
from jax import lax

BLK = 512
DH = 128
SEQ = 16384
NBLK = 32
HEADS = 16
D = 2048


def pair_fields(key):
    base = jax.random.fold_in(key, 11)
    key_q, key_k = jax.random.split(base, 2)
    query_field = jnp.clip(jax.random.normal(key_q, (SEQ, D), jnp.float32), -4.5, 4.5)
    key_field = jnp.clip(jax.random.normal(key_k, (SEQ, D), jnp.float32), -4.5, 4.5)
    return (query_field, key_field)


def draw_queries(key, part):
    return pair_fields(key)[0].astype(jnp.bfloat16)


def draw_keys(key, part):
    return pair_fields(key)[1].astype(jnp.bfloat16)


def draw_block_perm(key, part):
    base = jax.random.fold_in(key, 5)
    raw = jax.random.randint(base, (HEADS, NBLK), 0, 1 << 20)
    distinct = raw * NBLK + jnp.arange(NBLK, dtype=jnp.int32)[None, :]
    return jnp.argsort(distinct, axis=1, stable=True).astype(jnp.int32)


def steps_of(own_key, dims, shards, least, top_value):
    loudness = 1.0
    for position, parts in shards:
        heights = jax.random.uniform(jax.random.fold_in(jax.random.fold_in(own_key, 6), position), (parts,), jnp.float32, least / len(shards), top_value / len(shards))
        loudness = loudness * jnp.repeat(jnp.exp(heights), dims[position] // parts).reshape((-1,) + (1,) * (len(dims) - 1 - position))
    return loudness


def normal_values(own_key, dims, deviation, most, cuts=(), held_as=jnp.bfloat16):
    drawn = jax.random.normal(own_key, dims, jnp.float32) * deviation
    if len(cuts) > 0:
        drawn = steps_of(own_key, dims, cuts, -0.22, 0.18) * drawn
    return jnp.clip(drawn, min=-most, max=most).astype(held_as)


def setup_inputs(seed: int = 0) -> dict:
    key_of = jax.random.split(jax.random.key(seed), 6)
    queries = draw_queries(jax.random.fold_in(key_of[5], 71), 0)
    keys = draw_keys(jax.random.fold_in(key_of[5], 71), 0)
    values = normal_values(key_of[2], (SEQ, D), 1.0, 6.0, ((0, 32), (1, 16)))
    grad_out = normal_values(key_of[3], (SEQ, D), 1.0, 6.0, ((0, 32), (1, 16)))
    block_perm = draw_block_perm(jax.random.fold_in(key_of[5], 71), 0)
    return dict(queries=queries, keys=keys, values=values, grad_out=grad_out, block_perm=block_perm)


def window_block(query_rows, window, grad_rows, has_prev):
    width = query_rows.shape[1]
    span = query_rows.shape[0]
    scale = width ** -0.5
    win_keys = window[:, :width]
    win_values = window[:, width:]
    scores = jnp.dot(query_rows, win_keys.T, preferred_element_type=jnp.float32) * scale
    column = jnp.arange(window.shape[0], dtype=jnp.int32)
    allowed = jnp.logical_or(column >= span, has_prev)
    scores = jnp.where(allowed[None, :], scores, -1e30)
    top = jnp.max(scores, axis=1, keepdims=True)
    expon = jnp.exp(scores - top)
    probs = expon / jnp.sum(expon, axis=1, keepdims=True)
    probs_low = probs.astype(jnp.bfloat16)
    attended = jnp.dot(probs_low, win_values, preferred_element_type=jnp.float32).astype(jnp.bfloat16)
    grad_probs = jnp.dot(grad_rows, win_values.T, preferred_element_type=jnp.float32)
    delta = jnp.sum(probs * grad_probs, axis=1, keepdims=True)
    grad_scores = (probs * (grad_probs - delta) * scale).astype(jnp.bfloat16)
    grad_query = jnp.dot(grad_scores, win_keys, preferred_element_type=jnp.float32).astype(jnp.bfloat16)
    grad_key = jnp.dot(grad_scores.T, query_rows, preferred_element_type=jnp.float32)
    grad_value = jnp.dot(probs_low.T, grad_rows, preferred_element_type=jnp.float32)
    window_grads = jnp.concatenate([grad_key, grad_value], axis=1).astype(jnp.bfloat16)
    return attended, grad_query, window_grads


def head_pass(operands):
    query_head, key_head, value_head, grad_head, perm_row = operands
    pair = jnp.concatenate([key_head, value_head], axis=2)
    zero_block = jnp.zeros((1, BLK, 2 * DH), jnp.bfloat16)
    previous = jnp.concatenate([zero_block, pair[:-1]], axis=0)
    far_pair = jnp.take(pair, perm_row, axis=0)
    windows = jnp.concatenate([previous, pair, far_pair], axis=1)
    has_prev = jnp.arange(NBLK, dtype=jnp.int32) > 0

    def one_block(items):
        return window_block(items[0], items[1], items[2], items[3])

    attended, grad_query, window_grads = lax.map(one_block, (query_head, windows, grad_head, has_prev))
    local_part = window_grads[:, BLK:2 * BLK].astype(jnp.float32)
    prev_part = window_grads[:, :BLK].astype(jnp.float32)
    far_part = window_grads[:, 2 * BLK:].astype(jnp.float32)
    prev_moved = jnp.concatenate([prev_part[1:], jnp.zeros((1, BLK, 2 * DH), jnp.float32)], axis=0)
    far_moved = jnp.zeros((NBLK, BLK, 2 * DH), jnp.float32).at[perm_row].set(far_part)
    total = (local_part + prev_moved + far_moved).astype(jnp.bfloat16)
    return attended, grad_query, total[:, :, :DH], total[:, :, DH:]


def split_heads(array):
    return array.reshape(NBLK, BLK, HEADS, DH).transpose(2, 0, 1, 3)


def join_heads(array):
    return array.transpose(1, 2, 0, 3).reshape(SEQ, D)


def reference(queries, keys, values, grad_out, block_perm):
    results = lax.map(head_pass, (split_heads(queries), split_heads(keys), split_heads(values), split_heads(grad_out), block_perm))
    return (join_heads(results[0]), join_heads(results[1]), join_heads(results[2]), join_heads(results[3]))
```

```python
import jax
import jax.numpy as jnp
from jax import lax
from jax.sharding import PartitionSpec as P

BLK = 512


def passed_along(value, axis, steps):
    count = lax.axis_size(axis)
    first, last = (max(0, -steps), min(count, count - steps))
    return lax.ppermute(value, axis, [(source, source + steps) for source in range(first, last)])


def window_block(query_rows, window, grad_rows, has_prev):
    width = query_rows.shape[1]
    span = query_rows.shape[0]
    scale = width ** (-0.5)
    win_keys = window[:, :width]
    win_values = window[:, width:]
    scores = jnp.dot(query_rows, win_keys.T, preferred_element_type=jnp.float32) * scale
    column = jnp.arange(window.shape[0], dtype=jnp.int32)
    allowed = jnp.logical_or(column >= span, has_prev)
    scores = jnp.where(allowed[None, :], scores, -1e30)
    top = jnp.max(scores, axis=1, keepdims=True)
    expon = jnp.exp(scores - top)
    probs = expon / jnp.sum(expon, axis=1, keepdims=True)
    probs_low = probs.astype(jnp.bfloat16)
    attended = jnp.dot(probs_low, win_values, preferred_element_type=jnp.float32).astype(
        jnp.bfloat16
    )
    grad_probs = jnp.dot(grad_rows, win_values.T, preferred_element_type=jnp.float32)
    delta = jnp.sum(probs * grad_probs, axis=1, keepdims=True)
    grad_scores = (probs * (grad_probs - delta) * scale).astype(jnp.bfloat16)
    grad_query = jnp.dot(grad_scores, win_keys, preferred_element_type=jnp.float32).astype(
        jnp.bfloat16
    )
    grad_key = jnp.dot(grad_scores.T, query_rows, preferred_element_type=jnp.float32)
    grad_value = jnp.dot(probs_low.T, grad_rows, preferred_element_type=jnp.float32)
    window_grads = jnp.concatenate([grad_key, grad_value], axis=1).astype(jnp.bfloat16)
    return (attended, grad_query, window_grads)


def exchange(pieces):
    return lax.all_to_all(pieces, "seq", 0, 0, tiled=True)


def route(blocks, source_of):
    count = source_of.shape[0]
    pieces = blocks.reshape(count, blocks.shape[0] // count, blocks.shape[1])
    held = exchange(pieces)
    return exchange(jnp.take(held, source_of, axis=0)).reshape(blocks.shape)


def body(queries, keys, values, grad_out, block_perm):
    width = queries.shape[1]
    seq_index = lax.axis_index("seq")
    pair = jnp.concatenate([keys, values], axis=1)
    perm_row = block_perm[0]
    ids = jnp.arange(perm_row.shape[0], dtype=jnp.int32)
    inverse = jnp.sum(jnp.where(perm_row[None, :] == ids[:, None], ids[None, :], 0), axis=1)
    far_pair = route(pair, perm_row)
    prev_pair = passed_along(pair, "seq", 1)
    window = jnp.concatenate([prev_pair, pair, far_pair], axis=0)
    attended, grad_query, window_grads = window_block(queries, window, grad_out, seq_index > 0)
    far_back = route(window_grads[2 * BLK :], inverse)
    prev_back = passed_along(window_grads[:BLK], "seq", -1)
    total = (
        window_grads[BLK : 2 * BLK].astype(jnp.float32)
        + prev_back.astype(jnp.float32)
        + far_back.astype(jnp.float32)
    ).astype(jnp.bfloat16)
    return attended, grad_query, total[:, :width], total[:, width:]


def solution(mesh):
    placed = (
        P("seq", "head"),
        P("seq", "head"),
        P("seq", "head"),
        P("seq", "head"),
        P("head", None),
    )
    return jax.shard_map(
        body,
        mesh=mesh,
        in_specs=placed,
        out_specs=(P("seq", "head"), P("seq", "head"), P("seq", "head"), P("seq", "head")),
        check_vma=False,
    )
```

```python
import jax
import jax.numpy as jnp
from jax import lax
from jax.experimental import pallas as pl
from jax.experimental.pallas import tpu as pltpu
from jax.sharding import PartitionSpec as P

MESH = pl.DeviceIdType.MESH
AXIS = "seq"
ALONG_Z = 8


def dot_nt(left, right):
    return lax.dot_general(left, right, (((1,), (1,)), ((), ())), preferred_element_type=jnp.float32)


def dot_tn(left, right):
    return lax.dot_general(left, right, (((0,), (0,)), ((), ())), preferred_element_type=jnp.float32)


def dot_nn(left, right):
    return jnp.dot(left, right, preferred_element_type=jnp.float32)


def target(step, me, count):
    ring = step // (count // ALONG_Z)
    turn = (step + 1) % (count // ALONG_Z)
    along = (ALONG_Z // 2 + (1 - 2 * (ring % 2)) * ((ring + 1) // 2)) % ALONG_Z
    place = (me % ALONG_Z + along) % ALONG_Z
    row = (me // ALONG_Z + turn) % (count // ALONG_Z)
    return row * ALONG_Z + place


def rows_of(index, size):
    return pl.ds(pl.multiple_of(index * size, size), size)


def await_bytes(ref, sem):
    pltpu.make_async_copy(ref, ref, sem).wait()


def kernel(
    count, perm_ref, q_hbm, k_hbm, v_hbm, g_hbm, o_ref, dq_ref, dk_ref, dv_ref,
    inv, kv, qd, held_kv, held_qd, sorted_kv, sorted_qd, far_kv, far_qd, prev_kv, next_qd,
    stats, in_sem, send_sem, recv_sem,
):
    me = lax.axis_index(AXIS)
    span, width = q_hbm.shape
    piece = span // count
    scale = width ** (-0.5)
    others = count - 1

    loads = [
        pltpu.make_async_copy(k_hbm, kv.at[0], in_sem.at[0]),
        pltpu.make_async_copy(v_hbm, kv.at[1], in_sem.at[1]),
        pltpu.make_async_copy(q_hbm, qd.at[0], in_sem.at[2]),
        pltpu.make_async_copy(g_hbm, qd.at[1], in_sem.at[3]),
    ]
    for load in loads:
        load.start()

    barrier = pltpu.get_barrier_semaphore()

    def greet(step, carry):
        pl.semaphore_signal(
            barrier, inc=1, device_id={AXIS: target(step, me, count)}, device_id_type=MESH
        )
        return carry

    lax.fori_loop(0, others, greet, 0)

    def invert(block, carry):
        found = jnp.int32(0)
        for query in range(count):
            found = jnp.where(perm_ref[0, query] == block, query, found)
        inv[block] = found
        return carry

    lax.fori_loop(0, count, invert, 0)

    for load in loads:
        load.wait()
    pl.semaphore_wait(barrier, others)

    def spread(source, held, stream):
        def issue(step, carry):
            to = target(step, me, count)
            pltpu.make_async_remote_copy(
                src_ref=source.at[:, rows_of(to, piece), :],
                dst_ref=held.at[me],
                send_sem=send_sem.at[stream],
                recv_sem=recv_sem.at[stream],
                device_id={AXIS: to},
                device_id_type=MESH,
            ).start()
            return carry

        lax.fori_loop(0, others, issue, 0)

    def shift(source, landing, to, stream):
        return pltpu.make_async_remote_copy(
            src_ref=source,
            dst_ref=landing,
            send_sem=send_sem.at[stream],
            recv_sem=recv_sem.at[stream],
            device_id={AXIS: to},
            device_id_type=MESH,
        )

    def deliver(held, arranged, landing, index_of, stream_in, stream_out):
        held[me] = held_own[stream_in]
        await_bytes(held.at[pl.ds(0, others)], recv_sem.at[stream_in])

        def reorder(block, carry):
            arranged[block] = held[index_of(block)]
            return carry

        lax.fori_loop(0, count, reorder, 0)

        def issue(step, carry):
            to = target(step, me, count)
            pltpu.make_async_remote_copy(
                src_ref=arranged.at[to],
                dst_ref=landing.at[:, rows_of(me, piece), :],
                send_sem=send_sem.at[stream_out],
                recv_sem=recv_sem.at[stream_out],
                device_id={AXIS: to},
                device_id_type=MESH,
            ).start()
            return carry

        lax.fori_loop(0, others, issue, 0)
        landing[:, rows_of(me, piece), :] = arranged[me]

    shift_kv = shift(kv, prev_kv, (me + 1) % count, 2)
    shift_qd = shift(qd, next_qd, (me + count - 1) % count, 3)
    held_own = {0: kv[:, rows_of(me, piece), :], 1: qd[:, rows_of(me, piece), :]}

    spread(kv, held_kv, 0)

    @pl.when(me < others)
    def _():
        shift_kv.start()

    spread(qd, held_qd, 1)

    @pl.when(me > 0)
    def _():
        shift_qd.start()

    @pl.when(me == 0)
    def _():
        prev_kv[...] = jnp.zeros_like(prev_kv)

    @pl.when(me == others)
    def _():
        next_qd[...] = jnp.zeros_like(next_qd)

    deliver(held_kv, sorted_kv, far_kv, lambda block: perm_ref[0, block], 0, 4)
    deliver(held_qd, sorted_qd, far_qd, lambda block: inv[block], 1, 5)

    @pl.when(me > 0)
    def _():
        shift_kv.wait_recv()

    await_bytes(held_kv.at[pl.ds(0, others)], recv_sem.at[4])

    query_rows = qd[0]
    grad_rows = qd[1]
    key_sets = [prev_kv[0], kv[0], far_kv[0]]
    value_sets = [prev_kv[1], kv[1], far_kv[1]]
    scores = [dot_nt(keys, query_rows) * scale for keys in key_sets]
    scores[0] = jnp.where(me > 0, scores[0], -1e30)
    top = jnp.max(jnp.maximum(jnp.maximum(scores[0], scores[1]), scores[2]), axis=0, keepdims=True)
    expons = [jnp.exp(part - top) for part in scores]
    total = sum(jnp.sum(part, axis=0, keepdims=True) for part in expons)
    inverse_total = 1.0 / total
    probs = [part * inverse_total for part in expons]
    grad_probs = [dot_nt(values, grad_rows) for values in value_sets]
    delta = sum(
        jnp.sum(part * grads, axis=0, keepdims=True) for part, grads in zip(probs, grad_probs)
    )
    stats[me] = jnp.concatenate([top + jnp.log(total), delta], axis=0)
    attended = jnp.zeros((span, width), jnp.float32)
    grad_query = jnp.zeros((span, width), jnp.float32)
    for index in range(3):
        low = probs[index].astype(jnp.bfloat16)
        grad_scores = (probs[index] * (grad_probs[index] - delta) * scale).astype(jnp.bfloat16)
        attended += dot_tn(low, value_sets[index])
        grad_query += dot_tn(grad_scores, key_sets[index])
        if index == 1:
            grad_key = dot_nn(grad_scores, query_rows)
            grad_value = dot_nn(low, grad_rows)
    o_ref[...] = attended.astype(jnp.bfloat16)
    dq_ref[...] = grad_query.astype(jnp.bfloat16)

    def tell(step, carry):
        pltpu.make_async_remote_copy(
            src_ref=stats.at[me],
            dst_ref=stats.at[me],
            send_sem=send_sem.at[6],
            recv_sem=recv_sem.at[6],
            device_id={AXIS: target(step, me, count)},
            device_id_type=MESH,
        ).start()
        return carry

    lax.fori_loop(0, others, tell, 0)

    @pl.when(me < others)
    def _():
        shift_qd.wait_recv()

    await_bytes(held_qd.at[pl.ds(0, others)], recv_sem.at[5])
    await_bytes(stats.at[pl.ds(0, others)], recv_sem.at[6])

    known = {
        0: jnp.where(me < others, stats[(me + 1) % count], 0.0),
        1: stats[inv[me]],
    }
    for index, arrived in ((0, next_qd), (1, far_qd)):
        part_q = arrived[0]
        part_g = arrived[1]
        part = jnp.exp(dot_nt(kv[0], part_q) * scale - known[index][0:1])
        part_probs = dot_nt(kv[1], part_g)
        low = part.astype(jnp.bfloat16)
        grad_scores = (part * (part_probs - known[index][1:2]) * scale).astype(jnp.bfloat16)
        grad_key += dot_nn(grad_scores, part_q)
        grad_value += dot_nn(low, part_g)
    dk_ref[...] = grad_key.astype(jnp.bfloat16)
    dv_ref[...] = grad_value.astype(jnp.bfloat16)

    for stream, held in ((0, held_kv), (1, held_qd), (4, held_kv), (5, held_qd), (6, stats)):
        await_bytes(held.at[pl.ds(0, others)], send_sem.at[stream])

    @pl.when(me < others)
    def _():
        shift_kv.wait_send()

    @pl.when(me > 0)
    def _():
        shift_qd.wait_send()


def body(queries, keys, values, grad_out, block_perm):
    span, width = queries.shape
    count = lax.axis_size(AXIS)
    piece = span // count
    pair = pltpu.VMEM((2, span, width), jnp.bfloat16)
    pieces = pltpu.VMEM((count, 2, piece, width), jnp.bfloat16)
    in_place = pl.BlockSpec(memory_space=pl.ANY)
    in_vmem = pl.BlockSpec(memory_space=pltpu.VMEM)

    def run(*refs):
        kernel(count, *refs)

    return pl.pallas_call(
        run,
        out_shape=(jax.ShapeDtypeStruct((span, width), jnp.bfloat16),) * 4,
        in_specs=[pl.BlockSpec(memory_space=pltpu.SMEM), in_place, in_place, in_place, in_place],
        out_specs=(in_vmem,) * 4,
        scratch_shapes=[
            pltpu.SMEM((count,), jnp.int32),
            pair, pair, pieces, pieces, pieces, pieces, pair, pair, pair, pair,
            pltpu.VMEM((count, 2, span), jnp.float32),
            pltpu.SemaphoreType.DMA((4,)),
            pltpu.SemaphoreType.DMA((7,)),
            pltpu.SemaphoreType.DMA((7,)),
        ],
        compiler_params=pltpu.CompilerParams(
            collective_id=0, has_side_effects=True, vmem_limit_bytes=60 << 20
        ),
    )(block_perm, queries, keys, values, grad_out)


def solution(mesh):
    placed = (
        P("seq", "head"),
        P("seq", "head"),
        P("seq", "head"),
        P("seq", "head"),
        P("head", None),
    )
    return jax.shard_map(
        body,
        mesh=mesh,
        in_specs=placed,
        out_specs=(P("seq", "head"), P("seq", "head"), P("seq", "head"), P("seq", "head")),
        check_vma=False,
    )
```

```python
import jax
import jax.numpy as jnp
from jax import lax
from jax.experimental import pallas as pl
from jax.experimental.pallas import tpu as pltpu
from jax.sharding import PartitionSpec as P

MESH = pl.DeviceIdType.MESH
AXIS = "seq"
ALONG_Z = 8


def dot_nt(left, right):
    return lax.dot_general(left, right, (((1,), (1,)), ((), ())), preferred_element_type=jnp.float32)


def dot_tn(left, right):
    return lax.dot_general(left, right, (((0,), (0,)), ((), ())), preferred_element_type=jnp.float32)


def dot_nn(left, right):
    return jnp.dot(left, right, preferred_element_type=jnp.float32)


def target(step, me, count):
    ring = step // (count // ALONG_Z)
    turn = (step + 1) % (count // ALONG_Z)
    along = (ALONG_Z // 2 + (1 - 2 * (ring % 2)) * ((ring + 1) // 2)) % ALONG_Z
    place = (me % ALONG_Z + along) % ALONG_Z
    row = (me // ALONG_Z + turn) % (count // ALONG_Z)
    return row * ALONG_Z + place


def rows_of(index, size):
    return pl.ds(pl.multiple_of(index * size, size), size)


def await_bytes(ref, sem):
    pltpu.make_async_copy(ref, ref, sem).wait()


def kernel(
    count, perm_hbm, q_hbm, k_hbm, v_hbm, g_hbm, o_ref, dq_ref, dk_ref, dv_ref,
    perm_ref, inv, kv, qd, held_kv, held_qd, sorted_kv, sorted_qd, far_kv, far_qd, prev_kv, next_qd,
    full_stats, next_stats, part_stats, held_stats, sorted_stats, far_stats,
    in_sem, send_sem, recv_sem, up_sem, down_sem,
):
    me = lax.axis_index(AXIS)
    span, width = q_hbm.shape
    piece = span // count
    scale = width ** (-0.5)
    others = count - 1
    rows = count // ALONG_Z
    place = me % ALONG_Z
    row = me // ALONG_Z
    last = ALONG_Z - 1
    lanes = 128
    stat_rows = 2 * span // lanes
    stride = count // stat_rows

    def signal(sem, to):
        pl.semaphore_signal(sem, inc=1, device_id={AXIS: to}, device_id_type=MESH)

    def remote(source, landing, to, stream):
        return pltpu.make_async_remote_copy(
            src_ref=source,
            dst_ref=landing,
            send_sem=send_sem.at[stream],
            recv_sem=recv_sem.at[stream],
            device_id={AXIS: to},
            device_id_type=MESH,
        )

    barrier = pltpu.get_barrier_semaphore()
    for turn in range(1, rows):
        signal(barrier, (row + turn) % rows * ALONG_Z + place)

    @pl.when(place > 0)
    def _():
        signal(barrier, me - 1)

    @pl.when(place < last)
    def _():
        signal(barrier, me + 1)

    loads = [
        pltpu.make_async_copy(k_hbm, kv.at[0], in_sem.at[0]),
        pltpu.make_async_copy(v_hbm, kv.at[1], in_sem.at[1]),
        pltpu.make_async_copy(q_hbm, qd.at[0], in_sem.at[2]),
        pltpu.make_async_copy(g_hbm, qd.at[1], in_sem.at[3]),
        pltpu.make_async_copy(perm_hbm, perm_ref, in_sem.at[4]),
    ]
    for load in loads:
        load.start()

    greeted = rows - 1 + jnp.where(place > 0, 1, 0) + jnp.where(place < last, 1, 0)
    pl.semaphore_wait(barrier, greeted)

    @pl.when(place > 0)
    def _():
        signal(down_sem.at[0], me - 1)

    @pl.when(place < last)
    def _():
        signal(up_sem.at[0], me + 1)

    shift_kv = remote(kv, prev_kv, (me + 1) % count, 2)
    shift_qd = remote(qd, next_qd, (me + others) % count, 3)
    for load in loads[:2]:
        load.wait()

    @pl.when(place < last)
    def _():
        shift_kv.start()

    for load in loads[2:]:
        load.wait()

    @pl.when(place > 0)
    def _():
        shift_qd.start()

    def to_piece(source, held, to, stream):
        remote(source.at[:, rows_of(to, piece), :], held.at[me], to, stream).start()

    def to_column(there):
        for turn in range(rows):
            to_piece(kv, held_kv, (row + turn) % rows * ALONG_Z + there, 0)

    for turn in range(1, rows):
        to_piece(kv, held_kv, (row + turn) % rows * ALONG_Z + place, 0)

    def below(step, carry):
        pl.semaphore_wait(up_sem.at[step], 1)

        @pl.when(place < last)
        def _():
            signal(up_sem.at[step + 1], me + 1)

        to_column(place - 1 - step)
        return carry

    lax.fori_loop(0, place, below, 0)

    def above(step, carry):
        pl.semaphore_wait(down_sem.at[step], 1)

        @pl.when(place > 0)
        def _():
            signal(down_sem.at[step + 1], me - 1)

        to_column(place + 1 + step)
        return carry

    lax.fori_loop(0, last - place, above, 0)

    @pl.when((place == last) & (me < others))
    def _():
        shift_kv.start()

    def all_qd(step, carry):
        to_piece(qd, held_qd, target(step, me, count), 1)
        return carry

    lax.fori_loop(0, others, all_qd, 0)

    @pl.when((place == 0) & (me > 0))
    def _():
        shift_qd.start()

    def invert(block, carry):
        found = jnp.int32(0)
        for query in range(count):
            found = jnp.where(perm_ref[0, query] == block, query, found)
        inv[block] = found
        return carry

    lax.fori_loop(0, count, invert, 0)
    held_kv[me] = kv[:, rows_of(me, piece), :]
    held_qd[me] = qd[:, rows_of(me, piece), :]

    @pl.when(me == 0)
    def _():
        prev_kv[...] = jnp.zeros_like(prev_kv)

    @pl.when(me == others)
    def _():
        next_qd[...] = jnp.zeros_like(next_qd)
        next_stats[...] = jnp.zeros_like(next_stats)

    def arrange(held, arranged, index_of):
        def reorder(block, carry):
            arranged[block] = held[index_of(block)]
            return carry

        lax.fori_loop(0, count, reorder, 0)

    def deliver(arranged, landing, stream, first, end):
        def issue(step, carry):
            to = target(step, me, count)
            remote(arranged.at[to], landing.at[:, rows_of(me, piece), :], to, stream).start()
            return carry

        lax.fori_loop(first, end, issue, 0)

    query_rows = qd[0]
    grad_rows = qd[1]
    own_scores = dot_nt(kv[0], query_rows) * scale
    own_grads = dot_nt(kv[1], grad_rows)

    @pl.when(me > 0)
    def _():
        shift_kv.wait_recv()

    prev_scores = jnp.where(me > 0, dot_nt(prev_kv[0], query_rows) * scale, -1e30)
    prev_grads = dot_nt(prev_kv[1], grad_rows)
    near_top = jnp.max(jnp.maximum(own_scores, prev_scores), axis=0, keepdims=True)
    own_probs = jnp.exp(own_scores - near_top)
    prev_probs = jnp.exp(prev_scores - near_top)
    near_total = jnp.sum(own_probs + prev_probs, axis=0, keepdims=True)
    near_mass = near_top + jnp.log(near_total)
    near_delta = (
        jnp.sum(own_probs * own_grads + prev_probs * prev_grads, axis=0, keepdims=True) / near_total
    )
    for index in range(stat_rows):
        part = near_mass if index < stat_rows // 2 else near_delta
        start = index % (stat_rows // 2) * lanes
        part_stats[index] = part[:, start : start + lanes]

    for index in range(stat_rows):

        @pl.when(me != index * stride)
        def _():
            remote(part_stats.at[index], held_stats.at[me], index * stride, 6).start()

        @pl.when(me == index * stride)
        def _():
            held_stats[me] = part_stats[index]

    await_bytes(held_kv.at[pl.ds(0, others)], recv_sem.at[0])
    arrange(held_kv, sorted_kv, lambda block: perm_ref[0, block])
    deliver(sorted_kv, far_kv, 4, 0, others)
    far_kv[:, rows_of(me, piece), :] = sorted_kv[me]

    await_bytes(held_qd.at[pl.ds(0, others)], recv_sem.at[1])
    arrange(held_qd, sorted_qd, lambda block: inv[block])
    @pl.when(me % stride == 0)
    def _():
        await_bytes(held_stats.at[pl.ds(0, others)], recv_sem.at[6])
        arrange(held_stats, sorted_stats, lambda block: inv[block])

        def issue(step, carry):
            to = target(step, me, count)
            remote(sorted_stats.at[to], far_stats.at[me // stride], to, 8).start()
            return carry

        lax.fori_loop(0, others, issue, 0)
        far_stats[me // stride] = sorted_stats[me]

    deliver(sorted_qd, far_qd, 5, 0, count // 2)
    far_qd[:, rows_of(me, piece), :] = sorted_qd[me]

    await_bytes(held_kv.at[pl.ds(0, others)], recv_sem.at[4])

    far_scores = dot_nt(far_kv[0], query_rows) * scale
    far_grads = dot_nt(far_kv[1], grad_rows)
    far_top = jnp.max(far_scores, axis=0, keepdims=True)
    top = jnp.maximum(near_top, far_top)
    far_probs = jnp.exp(far_scores - top)
    near_weight = jnp.exp(near_top - top)
    total = near_total * near_weight + jnp.sum(far_probs, axis=0, keepdims=True)
    inverse_total = 1.0 / total
    near_weight = near_weight * inverse_total
    far_probs = far_probs * inverse_total
    delta = near_delta * near_total * near_weight + jnp.sum(
        far_probs * far_grads, axis=0, keepdims=True
    )
    full_stats[...] = jnp.concatenate([top + jnp.log(total), delta], axis=0)
    deliver(sorted_qd, far_qd, 5, count // 2, others)
    tell_prev = remote(full_stats, next_stats, (me + others) % count, 7)

    @pl.when(me > 0)
    def _():
        tell_prev.start()

    attended = jnp.zeros((span, width), jnp.float32)
    grad_query = jnp.zeros((span, width), jnp.float32)
    for probs, grads, pair, own in (
        (own_probs * near_weight, own_grads, kv, True),
        (prev_probs * near_weight, prev_grads, prev_kv, False),
        (far_probs, far_grads, far_kv, False),
    ):
        low = probs.astype(jnp.bfloat16)
        grad_scores = (probs * (grads - delta) * scale).astype(jnp.bfloat16)
        attended += dot_tn(low, pair[1])
        grad_query += dot_tn(grad_scores, pair[0])
        if own:
            grad_key = dot_nn(grad_scores, query_rows)
            grad_value = dot_nn(low, grad_rows)
    o_ref[...] = attended.astype(jnp.bfloat16)
    dq_ref[...] = grad_query.astype(jnp.bfloat16)

    @pl.when(me < others)
    def _():
        shift_qd.wait_recv()
        tell_prev.wait_recv()

    next_scores = dot_nt(kv[0], next_qd[0]) * scale
    next_grads = dot_nt(kv[1], next_qd[1])
    probs = jnp.exp(next_scores - next_stats[0:1])
    low = probs.astype(jnp.bfloat16)
    grad_scores = (probs * (next_grads - next_stats[1:2]) * scale).astype(jnp.bfloat16)
    grad_key += dot_nn(grad_scores, next_qd[0])
    grad_value += dot_nn(low, next_qd[1])

    await_bytes(held_qd.at[pl.ds(0, others)], recv_sem.at[5])

    @pl.when(me % stride == 0)
    def _():
        await_bytes(far_stats.at[pl.ds(0, stat_rows - 1)], recv_sem.at[8])

    @pl.when(me % stride != 0)
    def _():
        await_bytes(far_stats, recv_sem.at[8])

    half = stat_rows // 2
    mass = jnp.concatenate([far_stats[index] for index in range(half)], axis=1)
    seen = jnp.concatenate([far_stats[half + index] for index in range(half)], axis=1)
    scores = dot_nt(kv[0], far_qd[0]) * scale
    grads = dot_nt(kv[1], far_qd[1])
    top = jnp.maximum(mass, jnp.max(scores, axis=0, keepdims=True))
    probs = jnp.exp(scores - top)
    rest = jnp.exp(mass - top)
    inverse_total = 1.0 / (rest + jnp.sum(probs, axis=0, keepdims=True))
    probs = probs * inverse_total
    delta = seen * rest * inverse_total + jnp.sum(probs * grads, axis=0, keepdims=True)
    low = probs.astype(jnp.bfloat16)
    grad_scores = (probs * (grads - delta) * scale).astype(jnp.bfloat16)
    grad_key += dot_nn(grad_scores, far_qd[0])
    grad_value += dot_nn(low, far_qd[1])
    dk_ref[...] = grad_key.astype(jnp.bfloat16)
    dv_ref[...] = grad_value.astype(jnp.bfloat16)

    for stream, held in ((0, held_kv), (1, held_qd), (4, held_kv), (5, held_qd)):
        await_bytes(held.at[pl.ds(0, others)], send_sem.at[stream])

    @pl.when(me % stride == 0)
    def _():
        await_bytes(far_stats.at[pl.ds(0, stat_rows - 1)], send_sem.at[6])
        await_bytes(held_stats.at[pl.ds(0, others)], send_sem.at[8])

    @pl.when(me % stride != 0)
    def _():
        await_bytes(far_stats, send_sem.at[6])

    @pl.when(me < others)
    def _():
        shift_kv.wait_send()

    @pl.when(me > 0)
    def _():
        shift_qd.wait_send()
        tell_prev.wait_send()


def write_kernel(*refs):
    results, places, sem = refs[:4], refs[4:8], refs[8]
    copies = [
        pltpu.make_async_copy(result, place, sem.at[index])
        for index, (result, place) in enumerate(zip(results, places))
    ]
    for copy in copies:
        copy.start()
    for copy in copies:
        copy.wait()


def body(queries, keys, values, grad_out, block_perm):
    span, width = queries.shape
    count = lax.axis_size(AXIS)
    piece = span // count
    stat_rows = 2 * span // 128
    pair = pltpu.VMEM((2, span, width), jnp.bfloat16)
    pieces = pltpu.VMEM((count, 2, piece, width), jnp.bfloat16)
    in_place = pl.BlockSpec(memory_space=pltpu.HBM)
    in_vmem = pl.BlockSpec(memory_space=pltpu.VMEM)
    result = jax.ShapeDtypeStruct((span, width), jnp.bfloat16)

    def run(*refs):
        kernel(count, *refs)

    results = pl.pallas_call(
        run,
        out_shape=(pltpu.VMEM((span, width), jnp.bfloat16),) * 4,
        in_specs=[in_place] * 5,
        out_specs=(in_vmem,) * 4,
        scratch_shapes=[
            pltpu.SMEM((1, count), jnp.int32),
            pltpu.SMEM((count,), jnp.int32),
            pair, pair, pieces, pieces, pieces, pieces, pair, pair, pair, pair,
            pltpu.VMEM((2, span), jnp.float32),
            pltpu.VMEM((2, span), jnp.float32),
            pltpu.VMEM((stat_rows, 1, 128), jnp.float32),
            pltpu.VMEM((count, 1, 128), jnp.float32),
            pltpu.VMEM((count, 1, 128), jnp.float32),
            pltpu.VMEM((stat_rows, 1, 128), jnp.float32),
            pltpu.SemaphoreType.DMA((5,)),
            pltpu.SemaphoreType.DMA((9,)),
            pltpu.SemaphoreType.DMA((9,)),
            pltpu.SemaphoreType.REGULAR((ALONG_Z,)),
            pltpu.SemaphoreType.REGULAR((ALONG_Z,)),
        ],
        compiler_params=pltpu.CompilerParams(
            collective_id=0, has_side_effects=True, vmem_limit_bytes=66400000
        ),
    )(block_perm, queries, keys, values, grad_out)
    return pl.pallas_call(
        write_kernel,
        out_shape=(result,) * 4,
        in_specs=[in_vmem] * 4,
        out_specs=(in_place,) * 4,
        scratch_shapes=[pltpu.SemaphoreType.DMA((4,))],
    )(*(pltpu.with_memory_space_constraint(result, pltpu.VMEM) for result in results))


def solution(mesh):
    placed = (
        P("seq", "head"),
        P("seq", "head"),
        P("seq", "head"),
        P("seq", "head"),
        P("head", None),
    )
    return jax.shard_map(
        body,
        mesh=mesh,
        in_specs=placed,
        out_specs=(P("seq", "head"), P("seq", "head"), P("seq", "head"), P("seq", "head")),
        check_vma=False,
    )
```

```python
import jax
import jax.numpy as jnp
from jax import lax
from jax.experimental import pallas as pl
from jax.experimental.pallas import tpu as pltpu
from jax.sharding import PartitionSpec as P

MESH = pl.DeviceIdType.MESH
AXIS = "seq"
ALONG_Z = 8
QD_EARLY = 24
QD_FIRST = 16


def dot_nt(left, right):
    return lax.dot_general(left, right, (((1,), (1,)), ((), ())), preferred_element_type=jnp.float32)


def dot_tn(left, right):
    return lax.dot_general(left, right, (((0,), (0,)), ((), ())), preferred_element_type=jnp.float32)


def dot_nn(left, right):
    return jnp.dot(left, right, preferred_element_type=jnp.float32)


def target(step, me, count):
    ring = step // (count // ALONG_Z)
    turn = (step + 1) % (count // ALONG_Z)
    along = (ALONG_Z // 2 + (1 - 2 * (ring % 2)) * ((ring + 1) // 2)) % ALONG_Z
    place = (me % ALONG_Z + along) % ALONG_Z
    row = (me // ALONG_Z + turn) % (count // ALONG_Z)
    return row * ALONG_Z + place


def rows_of(index, size):
    return pl.ds(pl.multiple_of(index * size, size), size)


def await_bytes(ref, sem):
    pltpu.make_async_copy(ref, ref, sem).wait()


def kernel(
    count, perm_hbm, q_hbm, k_hbm, v_hbm, g_hbm, o_ref, dq_ref, dk_ref, dv_ref,
    perm_ref, inv, kv, qd, held_kv, held_qd, sorted_kv, sorted_qd, far_kv, far_qd, prev_kv, next_qd,
    full_stats, next_stats, part_stats, held_stats, sorted_stats, far_stats,
    in_sem, send_sem, recv_sem, up_sem, down_sem,
):
    me = lax.axis_index(AXIS)
    span, width = q_hbm.shape
    piece = span // count
    scale = width ** (-0.5)
    others = count - 1
    rows = count // ALONG_Z
    place = me % ALONG_Z
    row = me // ALONG_Z
    last = ALONG_Z - 1
    half = ALONG_Z // 2
    lanes = 128
    stat_rows = 2 * span // lanes
    stride = count // stat_rows

    def signal(sem, to):
        pl.semaphore_signal(sem, inc=1, device_id={AXIS: to}, device_id_type=MESH)

    def remote(source, landing, to, stream):
        return pltpu.make_async_remote_copy(
            src_ref=source,
            dst_ref=landing,
            send_sem=send_sem.at[stream],
            recv_sem=recv_sem.at[stream],
            device_id={AXIS: to},
            device_id_type=MESH,
        )

    barrier = pltpu.get_barrier_semaphore()
    for turn in range(1, rows):
        signal(barrier, (row + turn) % rows * ALONG_Z + place)

    @pl.when(place > 0)
    def _():
        signal(barrier, me - 1)

    @pl.when(place < last)
    def _():
        signal(barrier, me + 1)

    loads = [
        pltpu.make_async_copy(k_hbm, kv.at[0], in_sem.at[0]),
        pltpu.make_async_copy(v_hbm, kv.at[1], in_sem.at[1]),
        pltpu.make_async_copy(q_hbm, qd.at[0], in_sem.at[2]),
        pltpu.make_async_copy(g_hbm, qd.at[1], in_sem.at[3]),
        pltpu.make_async_copy(perm_hbm, perm_ref, in_sem.at[4]),
    ]
    for load in loads:
        load.start()

    greeted = rows - 1 + jnp.where(place > 0, 1, 0) + jnp.where(place < last, 1, 0)
    pl.semaphore_wait(barrier, greeted)

    @pl.when(place > 0)
    def _():
        signal(down_sem.at[0], me - 1)

    @pl.when(place < last)
    def _():
        signal(up_sem.at[0], me + 1)

    shift_kv = remote(kv, prev_kv, (me + 1) % count, 2)
    shift_qd = remote(qd, next_qd, (me + others) % count, 3)
    for load in loads[:2]:
        load.wait()

    @pl.when(place < last)
    def _():
        shift_kv.start()

    def to_piece(source, held, to, stream):
        remote(source.at[:, rows_of(to, piece), :], held.at[me], to, stream).start()

    def to_column(there):
        for turn in range(rows):
            to_piece(kv, held_kv, (row + turn) % rows * ALONG_Z + there, 0)

    for turn in range(1, rows):
        to_piece(kv, held_kv, (row + turn) % rows * ALONG_Z + place, 0)

    def below(step, carry):
        pl.semaphore_wait(up_sem.at[step], 1)

        @pl.when(place < last)
        def _():
            signal(up_sem.at[step + 1], me + 1)

        to_column(place - 1 - step)
        return carry

    lax.fori_loop(0, place, below, 0)

    def above(step, carry):
        pl.semaphore_wait(down_sem.at[step], 1)

        @pl.when(place > 0)
        def _():
            signal(down_sem.at[step + 1], me - 1)

        to_column(place + 1 + step)
        return carry

    lax.fori_loop(0, last - place, above, 0)

    @pl.when((place == last) & (me < others))
    def _():
        shift_kv.start()

    for load in loads[2:]:
        load.wait()

    own_side = place // half * half

    def near_rows(index):
        start = (index * ALONG_Z + own_side) * piece
        return pl.ds(pl.multiple_of(start, half * piece), half * piece)

    crosses = (place == half) | ((place == 0) & (me > 0))

    def shift_part(index):
        part = (slice(None), near_rows(index), slice(None))
        return remote(qd.at[part], next_qd.at[part], (me + others) % count, 3)

    @pl.when(crosses)
    def _():
        for index in range(rows):
            shift_part(index).start()

    @pl.when((place > 0) & (place != half))
    def _():
        shift_qd.start()
    def all_qd(step, carry):
        to_piece(qd, held_qd, target(step, me, count), 1)
        return carry

    @pl.when(place == 0)
    def _():
        lax.fori_loop(0, QD_FIRST, all_qd, 0)

    def invert(block, carry):
        found = jnp.int32(0)
        for query in range(count):
            found = jnp.where(perm_ref[0, query] == block, query, found)
        inv[block] = found
        return carry

    lax.fori_loop(0, count, invert, 0)
    held_kv[me] = kv[:, rows_of(me, piece), :]
    held_qd[me] = qd[:, rows_of(me, piece), :]

    @pl.when(me == 0)
    def _():
        prev_kv[...] = jnp.zeros_like(prev_kv)

    @pl.when(me == others)
    def _():
        next_qd[...] = jnp.zeros_like(next_qd)
        next_stats[...] = jnp.zeros_like(next_stats)

    def arrange(held, arranged, index_of):
        def reorder(block, carry):
            arranged[block] = held[index_of(block)]
            return carry

        lax.fori_loop(0, count, reorder, 0)

    def deliver(arranged, landing, stream, first, end):
        def issue(step, carry):
            to = target(step, me, count)
            remote(arranged.at[to], landing.at[:, rows_of(me, piece), :], to, stream).start()
            return carry

        lax.fori_loop(first, end, issue, 0)

    query_rows = qd[0]
    grad_rows = qd[1]
    own_scores = dot_nt(kv[0], query_rows) * scale
    own_grads = dot_nt(kv[1], grad_rows)

    @pl.when(me > 0)
    def _():
        shift_kv.wait_recv()

    prev_scores = jnp.where(me > 0, dot_nt(prev_kv[0], query_rows) * scale, -1e30)
    prev_grads = dot_nt(prev_kv[1], grad_rows)
    near_top = jnp.max(jnp.maximum(own_scores, prev_scores), axis=0, keepdims=True)
    own_probs = jnp.exp(own_scores - near_top)
    prev_probs = jnp.exp(prev_scores - near_top)
    near_total = jnp.sum(own_probs + prev_probs, axis=0, keepdims=True)
    near_mass = near_top + jnp.log(near_total)
    near_delta = (
        jnp.sum(own_probs * own_grads + prev_probs * prev_grads, axis=0, keepdims=True) / near_total
    )
    for index in range(stat_rows):
        part = near_mass if index < stat_rows // 2 else near_delta
        start = index % (stat_rows // 2) * lanes
        part_stats[index] = part[:, start : start + lanes]

    for index in range(stat_rows):

        @pl.when(me != index * stride)
        def _():
            remote(part_stats.at[index], held_stats.at[me], index * stride, 6).start()

        @pl.when(me == index * stride)
        def _():
            held_stats[me] = part_stats[index]

    lax.fori_loop(jnp.where(place == 0, QD_FIRST, 0), others, all_qd, 0)

    await_bytes(held_kv.at[pl.ds(0, others)], recv_sem.at[0])
    arrange(held_kv, sorted_kv, lambda block: perm_ref[0, block])
    deliver(sorted_kv, far_kv, 4, 0, others)
    far_kv[:, rows_of(me, piece), :] = sorted_kv[me]

    await_bytes(held_qd.at[pl.ds(0, others)], recv_sem.at[1])
    arrange(held_qd, sorted_qd, lambda block: inv[block])
    @pl.when(me % stride == 0)
    def _():
        await_bytes(held_stats.at[pl.ds(0, others)], recv_sem.at[6])
        arrange(held_stats, sorted_stats, lambda block: inv[block])

        def issue(step, carry):
            to = target(step, me, count)
            remote(sorted_stats.at[to], far_stats.at[me // stride], to, 8).start()
            return carry

        lax.fori_loop(0, others, issue, 0)
        far_stats[me // stride] = sorted_stats[me]

    def forward(index):
        there = index * ALONG_Z + jnp.where(place < half, half - 1, last)
        origin = there + 1
        part = (slice(None), rows_of(me, piece), slice(None))
        meant = (origin < count) & (there != me)
        return meant, pltpu.make_async_remote_copy(
            src_ref=held_qd.at[origin % count],
            dst_ref=next_qd.at[part],
            send_sem=send_sem.at[9],
            recv_sem=recv_sem.at[3],
            device_id={AXIS: there},
            device_id_type=MESH,
        )

    for index in range(rows):
        meant, copy = forward(index)

        @pl.when(meant)
        def _():
            copy.start()

    @pl.when(((place == half - 1) | (place == last)) & (me < others))
    def _():
        next_qd[:, rows_of(me, piece), :] = held_qd[(me + 1) % count]

    deliver(sorted_qd, far_qd, 5, 0, QD_EARLY)
    far_qd[:, rows_of(me, piece), :] = sorted_qd[me]

    await_bytes(held_kv.at[pl.ds(0, others)], recv_sem.at[4])

    far_scores = dot_nt(far_kv[0], query_rows) * scale
    far_grads = dot_nt(far_kv[1], grad_rows)
    far_top = jnp.max(far_scores, axis=0, keepdims=True)
    top = jnp.maximum(near_top, far_top)
    far_probs = jnp.exp(far_scores - top)
    near_weight = jnp.exp(near_top - top)
    total = near_total * near_weight + jnp.sum(far_probs, axis=0, keepdims=True)
    inverse_total = 1.0 / total
    near_weight = near_weight * inverse_total
    far_probs = far_probs * inverse_total
    delta = near_delta * near_total * near_weight + jnp.sum(
        far_probs * far_grads, axis=0, keepdims=True
    )
    full_stats[...] = jnp.concatenate([top + jnp.log(total), delta], axis=0)
    deliver(sorted_qd, far_qd, 5, QD_EARLY, others)
    tell_prev = remote(full_stats, next_stats, (me + others) % count, 7)

    @pl.when(me > 0)
    def _():
        tell_prev.start()

    attended = jnp.zeros((span, width), jnp.float32)
    grad_query = jnp.zeros((span, width), jnp.float32)
    for probs, grads, pair, own in (
        (own_probs * near_weight, own_grads, kv, True),
        (prev_probs * near_weight, prev_grads, prev_kv, False),
        (far_probs, far_grads, far_kv, False),
    ):
        low = probs.astype(jnp.bfloat16)
        grad_scores = (probs * (grads - delta) * scale).astype(jnp.bfloat16)
        attended += dot_tn(low, pair[1])
        grad_query += dot_tn(grad_scores, pair[0])
        if own:
            grad_key = dot_nn(grad_scores, query_rows)
            grad_value = dot_nn(low, grad_rows)
    o_ref[...] = attended.astype(jnp.bfloat16)
    dq_ref[...] = grad_query.astype(jnp.bfloat16)

    gathers = ((place == half - 1) | (place == last)) & (me < others)

    @pl.when(gathers)
    def _():
        await_bytes(next_qd.at[:, pl.ds(0, span - piece), :], recv_sem.at[3])

    @pl.when((place != half - 1) & (place != last))
    def _():
        shift_qd.wait_recv()
    @pl.when(me < others)
    def _():
        tell_prev.wait_recv()

    next_scores = dot_nt(kv[0], next_qd[0]) * scale
    next_grads = dot_nt(kv[1], next_qd[1])
    probs = jnp.exp(next_scores - next_stats[0:1])
    low = probs.astype(jnp.bfloat16)
    grad_scores = (probs * (next_grads - next_stats[1:2]) * scale).astype(jnp.bfloat16)
    grad_key += dot_nn(grad_scores, next_qd[0])
    grad_value += dot_nn(low, next_qd[1])

    await_bytes(held_qd.at[pl.ds(0, others)], recv_sem.at[5])

    @pl.when(me % stride == 0)
    def _():
        await_bytes(far_stats.at[pl.ds(0, stat_rows - 1)], recv_sem.at[8])

    @pl.when(me % stride != 0)
    def _():
        await_bytes(far_stats, recv_sem.at[8])

    stat_half = stat_rows // 2
    mass = jnp.concatenate([far_stats[index] for index in range(stat_half)], axis=1)
    seen = jnp.concatenate([far_stats[stat_half + index] for index in range(stat_half)], axis=1)
    scores = dot_nt(kv[0], far_qd[0]) * scale
    grads = dot_nt(kv[1], far_qd[1])
    top = jnp.maximum(mass, jnp.max(scores, axis=0, keepdims=True))
    probs = jnp.exp(scores - top)
    rest = jnp.exp(mass - top)
    inverse_total = 1.0 / (rest + jnp.sum(probs, axis=0, keepdims=True))
    probs = probs * inverse_total
    delta = seen * rest * inverse_total + jnp.sum(probs * grads, axis=0, keepdims=True)
    low = probs.astype(jnp.bfloat16)
    grad_scores = (probs * (grads - delta) * scale).astype(jnp.bfloat16)
    grad_key += dot_nn(grad_scores, far_qd[0])
    grad_value += dot_nn(low, far_qd[1])
    dk_ref[...] = grad_key.astype(jnp.bfloat16)
    dv_ref[...] = grad_value.astype(jnp.bfloat16)

    for stream, held in ((0, held_kv), (1, held_qd), (4, held_kv), (5, held_qd)):
        await_bytes(held.at[pl.ds(0, others)], send_sem.at[stream])

    @pl.when(me % stride == 0)
    def _():
        await_bytes(far_stats.at[pl.ds(0, stat_rows - 1)], send_sem.at[6])
        await_bytes(held_stats.at[pl.ds(0, others)], send_sem.at[8])

    @pl.when(me % stride != 0)
    def _():
        await_bytes(far_stats, send_sem.at[6])

    @pl.when(me < others)
    def _():
        shift_kv.wait_send()


    @pl.when(crosses)
    def _():
        await_bytes(next_qd.at[:, pl.ds(0, span // 2), :], send_sem.at[3])

    @pl.when((place > 0) & (place != half))
    def _():
        shift_qd.wait_send()

    for index in range(rows):
        meant, copy = forward(index)

        @pl.when(meant)
        def _():
            copy.wait_send()
    @pl.when(me > 0)
    def _():
        tell_prev.wait_send()


def write_kernel(*refs):
    results, places, sem = refs[:4], refs[4:8], refs[8]
    copies = [
        pltpu.make_async_copy(result, place, sem.at[index])
        for index, (result, place) in enumerate(zip(results, places))
    ]
    for copy in copies:
        copy.start()
    for copy in copies:
        copy.wait()


def body(queries, keys, values, grad_out, block_perm):
    span, width = queries.shape
    count = lax.axis_size(AXIS)
    piece = span // count
    stat_rows = 2 * span // 128
    pair = pltpu.VMEM((2, span, width), jnp.bfloat16)
    pieces = pltpu.VMEM((count, 2, piece, width), jnp.bfloat16)
    in_place = pl.BlockSpec(memory_space=pltpu.HBM)
    in_vmem = pl.BlockSpec(memory_space=pltpu.VMEM)
    result = jax.ShapeDtypeStruct((span, width), jnp.bfloat16)

    def run(*refs):
        kernel(count, *refs)

    results = pl.pallas_call(
        run,
        out_shape=(pltpu.VMEM((span, width), jnp.bfloat16),) * 4,
        in_specs=[in_place] * 5,
        out_specs=(in_vmem,) * 4,
        scratch_shapes=[
            pltpu.SMEM((1, count), jnp.int32),
            pltpu.SMEM((count,), jnp.int32),
            pair, pair, pieces, pieces, pieces, pieces, pair, pair, pair, pair,
            pltpu.VMEM((2, span), jnp.float32),
            pltpu.VMEM((2, span), jnp.float32),
            pltpu.VMEM((stat_rows, 1, 128), jnp.float32),
            pltpu.VMEM((count, 1, 128), jnp.float32),
            pltpu.VMEM((count, 1, 128), jnp.float32),
            pltpu.VMEM((stat_rows, 1, 128), jnp.float32),
            pltpu.SemaphoreType.DMA((5,)),
            pltpu.SemaphoreType.DMA((10,)),
            pltpu.SemaphoreType.DMA((9,)),
            pltpu.SemaphoreType.REGULAR((ALONG_Z,)),
            pltpu.SemaphoreType.REGULAR((ALONG_Z,)),
        ],
        compiler_params=pltpu.CompilerParams(
            collective_id=0, has_side_effects=True, vmem_limit_bytes=66400000
        ),
    )(block_perm, queries, keys, values, grad_out)
    return pl.pallas_call(
        write_kernel,
        out_shape=(result,) * 4,
        in_specs=[in_vmem] * 4,
        out_specs=(in_place,) * 4,
        scratch_shapes=[pltpu.SemaphoreType.DMA((4,))],
    )(*(pltpu.with_memory_space_constraint(result, pltpu.VMEM) for result in results))


def solution(mesh):
    placed = (
        P("seq", "head"),
        P("seq", "head"),
        P("seq", "head"),
        P("seq", "head"),
        P("head", None),
    )
    return jax.shard_map(
        body,
        mesh=mesh,
        in_specs=placed,
        out_specs=(P("seq", "head"), P("seq", "head"), P("seq", "head"), P("seq", "head")),
        check_vma=False,
    )
```

```python
import jax
import jax.numpy as jnp
from jax import lax
from jax.experimental import pallas as pl
from jax.experimental.pallas import tpu as pltpu
from jax.sharding import PartitionSpec as P

MESH = pl.DeviceIdType.MESH
AXIS = "seq"
ALONG_Z = 8
QD_EARLY = 24
QD_FIRST = 16


def dot_nt(left, right):
    return lax.dot_general(left, right, (((1,), (1,)), ((), ())), preferred_element_type=jnp.float32)


def dot_tn(left, right):
    return lax.dot_general(left, right, (((0,), (0,)), ((), ())), preferred_element_type=jnp.float32)


def dot_nn(left, right):
    return jnp.dot(left, right, preferred_element_type=jnp.float32)


def target(step, me, count):
    ring = step // (count // ALONG_Z)
    turn = (step + 1) % (count // ALONG_Z)
    along = (ALONG_Z // 2 + (1 - 2 * (ring % 2)) * ((ring + 1) // 2)) % ALONG_Z
    place = (me % ALONG_Z + along) % ALONG_Z
    row = (me // ALONG_Z + turn) % (count // ALONG_Z)
    return row * ALONG_Z + place


def outward(step, me, count):
    ring = step // (count // ALONG_Z)
    turn = step % (count // ALONG_Z)
    place = (ring % 2) * (ALONG_Z - 1) + (1 - 2 * (ring % 2)) * (ring // 2)
    row = (me // ALONG_Z + turn) % (count // ALONG_Z)
    return row * ALONG_Z + place


def rows_of(index, size):
    return pl.ds(pl.multiple_of(index * size, size), size)


def await_bytes(ref, sem):
    pltpu.make_async_copy(ref, ref, sem).wait()


def kernel(
    count, perm_hbm, q_hbm, k_hbm, v_hbm, g_hbm, o_ref, dq_ref, dk_ref, dv_ref,
    perm_ref, inv, kv, qd, held_kv, held_qd, sorted_kv, sorted_qd, far_kv, far_qd, prev_kv, next_qd,
    full_stats, next_stats, part_stats, held_stats, sorted_stats, far_stats,
    in_sem, send_sem, recv_sem, up_sem, down_sem,
):
    me = lax.axis_index(AXIS)
    span, width = q_hbm.shape
    piece = span // count
    scale = width ** (-0.5)
    others = count - 1
    rows = count // ALONG_Z
    place = me % ALONG_Z
    row = me // ALONG_Z
    last = ALONG_Z - 1
    half = ALONG_Z // 2
    lanes = 128
    stat_rows = 2 * span // lanes
    stride = count // stat_rows

    def signal(sem, to):
        pl.semaphore_signal(sem, inc=1, device_id={AXIS: to}, device_id_type=MESH)

    def remote(source, landing, to, stream):
        return pltpu.make_async_remote_copy(
            src_ref=source,
            dst_ref=landing,
            send_sem=send_sem.at[stream],
            recv_sem=recv_sem.at[stream],
            device_id={AXIS: to},
            device_id_type=MESH,
        )

    barrier = pltpu.get_barrier_semaphore()
    for turn in range(1, rows):
        signal(barrier, (row + turn) % rows * ALONG_Z + place)

    @pl.when(place > 0)
    def _():
        signal(barrier, me - 1)

    @pl.when(place < last)
    def _():
        signal(barrier, me + 1)

    loads = [
        pltpu.make_async_copy(k_hbm, kv.at[0], in_sem.at[0]),
        pltpu.make_async_copy(v_hbm, kv.at[1], in_sem.at[1]),
        pltpu.make_async_copy(q_hbm, qd.at[0], in_sem.at[2]),
        pltpu.make_async_copy(g_hbm, qd.at[1], in_sem.at[3]),
        pltpu.make_async_copy(perm_hbm, perm_ref, in_sem.at[4]),
    ]
    for load in loads:
        load.start()

    greeted = rows - 1 + jnp.where(place > 0, 1, 0) + jnp.where(place < last, 1, 0)
    pl.semaphore_wait(barrier, greeted)

    @pl.when(place > 0)
    def _():
        signal(down_sem.at[0], me - 1)

    @pl.when(place < last)
    def _():
        signal(up_sem.at[0], me + 1)

    shift_kv = remote(kv, prev_kv, (me + 1) % count, 2)
    shift_qd = remote(qd, next_qd, (me + others) % count, 3)
    for load in loads[:2]:
        load.wait()

    @pl.when(place < last)
    def _():
        shift_kv.start()

    def to_piece(source, held, to, stream):
        remote(source.at[:, rows_of(to, piece), :], held.at[me], to, stream).start()

    def to_column(there):
        for turn in range(rows):
            to_piece(kv, held_kv, (row + turn) % rows * ALONG_Z + there, 0)

    for turn in range(1, rows):
        to_piece(kv, held_kv, (row + turn) % rows * ALONG_Z + place, 0)

    def below(step, carry):
        pl.semaphore_wait(up_sem.at[step], 1)

        @pl.when(place < last)
        def _():
            signal(up_sem.at[step + 1], me + 1)

        to_column(place - 1 - step)
        return carry

    lax.fori_loop(0, place, below, 0)

    def above(step, carry):
        pl.semaphore_wait(down_sem.at[step], 1)

        @pl.when(place > 0)
        def _():
            signal(down_sem.at[step + 1], me - 1)

        to_column(place + 1 + step)
        return carry

    lax.fori_loop(0, last - place, above, 0)

    @pl.when((place == last) & (me < others))
    def _():
        shift_kv.start()

    for load in loads[2:]:
        load.wait()

    own_side = place // half * half

    def near_rows(index):
        start = (index * ALONG_Z + own_side) * piece
        return pl.ds(pl.multiple_of(start, half * piece), half * piece)

    crosses = (place == half) | ((place == 0) & (me > 0))

    def shift_part(index):
        part = (slice(None), near_rows(index), slice(None))
        return remote(qd.at[part], next_qd.at[part], (me + others) % count, 3)

    def all_qd(step, carry):
        to_piece(qd, held_qd, target(step, me, count), 1)
        return carry

    @pl.when(place == 0)
    def _():
        lax.fori_loop(0, QD_FIRST, all_qd, 0)

    def invert(block, carry):
        found = jnp.int32(0)
        for query in range(count):
            found = jnp.where(perm_ref[0, query] == block, query, found)
        inv[block] = found
        return carry

    lax.fori_loop(0, count, invert, 0)
    held_kv[me] = kv[:, rows_of(me, piece), :]
    held_qd[me] = qd[:, rows_of(me, piece), :]

    @pl.when(me == 0)
    def _():
        prev_kv[...] = jnp.zeros_like(prev_kv)

    @pl.when(me == others)
    def _():
        next_qd[...] = jnp.zeros_like(next_qd)
        next_stats[...] = jnp.zeros_like(next_stats)

    def arrange(held, arranged, index_of):
        def reorder(block, carry):
            arranged[block] = held[index_of(block)]
            return carry

        lax.fori_loop(0, count, reorder, 0)

    def deliver(arranged, landing, stream, first, end):
        def issue(step, carry):
            to = outward(step, me, count)

            @pl.when(to != me)
            def _():
                remote(arranged.at[to], landing.at[:, rows_of(me, piece), :], to, stream).start()

            return carry

        lax.fori_loop(first, end, issue, 0)

    query_rows = qd[0]
    grad_rows = qd[1]
    own_scores = dot_nt(kv[0], query_rows) * scale
    own_grads = dot_nt(kv[1], grad_rows)

    @pl.when(me > 0)
    def _():
        shift_kv.wait_recv()

    prev_scores = jnp.where(me > 0, dot_nt(prev_kv[0], query_rows) * scale, -1e30)
    prev_grads = dot_nt(prev_kv[1], grad_rows)
    near_top = jnp.max(jnp.maximum(own_scores, prev_scores), axis=0, keepdims=True)
    own_probs = jnp.exp(own_scores - near_top)
    prev_probs = jnp.exp(prev_scores - near_top)
    near_total = jnp.sum(own_probs + prev_probs, axis=0, keepdims=True)
    near_mass = near_top + jnp.log(near_total)
    near_delta = (
        jnp.sum(own_probs * own_grads + prev_probs * prev_grads, axis=0, keepdims=True) / near_total
    )
    for index in range(stat_rows):
        part = near_mass if index < stat_rows // 2 else near_delta
        start = index % (stat_rows // 2) * lanes
        part_stats[index] = part[:, start : start + lanes]

    for index in range(stat_rows):

        @pl.when(me != index * stride)
        def _():
            remote(part_stats.at[index], held_stats.at[me], index * stride, 6).start()

        @pl.when(me == index * stride)
        def _():
            held_stats[me] = part_stats[index]

    lax.fori_loop(jnp.where(place == 0, QD_FIRST, 0), others, all_qd, 0)

    await_bytes(held_kv.at[pl.ds(0, others)], recv_sem.at[0])
    arrange(held_kv, sorted_kv, lambda block: perm_ref[0, block])
    deliver(sorted_kv, far_kv, 4, 0, count)
    far_kv[:, rows_of(me, piece), :] = sorted_kv[me]

    @pl.when(crosses)
    def _():
        for index in range(rows):
            shift_part(index).start()

    @pl.when((place > 0) & (place != half))
    def _():
        shift_qd.start()
    await_bytes(held_qd.at[pl.ds(0, others)], recv_sem.at[1])
    arrange(held_qd, sorted_qd, lambda block: inv[block])
    @pl.when(me % stride == 0)
    def _():
        await_bytes(held_stats.at[pl.ds(0, others)], recv_sem.at[6])
        arrange(held_stats, sorted_stats, lambda block: inv[block])

        def issue(step, carry):
            to = target(step, me, count)
            remote(sorted_stats.at[to], far_stats.at[me // stride], to, 8).start()
            return carry

        lax.fori_loop(0, others, issue, 0)
        far_stats[me // stride] = sorted_stats[me]

    def forward(index):
        there = index * ALONG_Z + jnp.where(place < half, half - 1, last)
        origin = there + 1
        part = (slice(None), rows_of(me, piece), slice(None))
        meant = (origin < count) & (there != me)
        return meant, pltpu.make_async_remote_copy(
            src_ref=held_qd.at[origin % count],
            dst_ref=next_qd.at[part],
            send_sem=send_sem.at[9],
            recv_sem=recv_sem.at[3],
            device_id={AXIS: there},
            device_id_type=MESH,
        )

    for index in range(rows):
        meant, copy = forward(index)

        @pl.when(meant)
        def _():
            copy.start()

    @pl.when(((place == half - 1) | (place == last)) & (me < others))
    def _():
        next_qd[:, rows_of(me, piece), :] = held_qd[(me + 1) % count]

    deliver(sorted_qd, far_qd, 5, 0, QD_EARLY)
    far_qd[:, rows_of(me, piece), :] = sorted_qd[me]

    await_bytes(held_kv.at[pl.ds(0, others)], recv_sem.at[4])

    far_scores = dot_nt(far_kv[0], query_rows) * scale
    far_grads = dot_nt(far_kv[1], grad_rows)
    far_top = jnp.max(far_scores, axis=0, keepdims=True)
    top = jnp.maximum(near_top, far_top)
    far_probs = jnp.exp(far_scores - top)
    near_weight = jnp.exp(near_top - top)
    total = near_total * near_weight + jnp.sum(far_probs, axis=0, keepdims=True)
    inverse_total = 1.0 / total
    near_weight = near_weight * inverse_total
    far_probs = far_probs * inverse_total
    delta = near_delta * near_total * near_weight + jnp.sum(
        far_probs * far_grads, axis=0, keepdims=True
    )
    full_stats[...] = jnp.concatenate([top + jnp.log(total), delta], axis=0)
    deliver(sorted_qd, far_qd, 5, QD_EARLY, count)
    tell_prev = remote(full_stats, next_stats, (me + others) % count, 7)

    @pl.when(me > 0)
    def _():
        tell_prev.start()

    attended = jnp.zeros((span, width), jnp.float32)
    grad_query = jnp.zeros((span, width), jnp.float32)
    for probs, grads, pair, own in (
        (own_probs * near_weight, own_grads, kv, True),
        (prev_probs * near_weight, prev_grads, prev_kv, False),
        (far_probs, far_grads, far_kv, False),
    ):
        low = probs.astype(jnp.bfloat16)
        grad_scores = (probs * (grads - delta) * scale).astype(jnp.bfloat16)
        attended += dot_tn(low, pair[1])
        grad_query += dot_tn(grad_scores, pair[0])
        if own:
            grad_key = dot_nn(grad_scores, query_rows)
            grad_value = dot_nn(low, grad_rows)
    o_ref[...] = attended.astype(jnp.bfloat16)
    dq_ref[...] = grad_query.astype(jnp.bfloat16)

    gathers = ((place == half - 1) | (place == last)) & (me < others)

    @pl.when(gathers)
    def _():
        await_bytes(next_qd.at[:, pl.ds(0, span - piece), :], recv_sem.at[3])

    @pl.when((place != half - 1) & (place != last))
    def _():
        shift_qd.wait_recv()
    @pl.when(me < others)
    def _():
        tell_prev.wait_recv()

    next_scores = dot_nt(kv[0], next_qd[0]) * scale
    next_grads = dot_nt(kv[1], next_qd[1])
    probs = jnp.exp(next_scores - next_stats[0:1])
    low = probs.astype(jnp.bfloat16)
    grad_scores = (probs * (next_grads - next_stats[1:2]) * scale).astype(jnp.bfloat16)
    grad_key += dot_nn(grad_scores, next_qd[0])
    grad_value += dot_nn(low, next_qd[1])

    await_bytes(held_qd.at[pl.ds(0, others)], recv_sem.at[5])

    @pl.when(me % stride == 0)
    def _():
        await_bytes(far_stats.at[pl.ds(0, stat_rows - 1)], recv_sem.at[8])

    @pl.when(me % stride != 0)
    def _():
        await_bytes(far_stats, recv_sem.at[8])

    stat_half = stat_rows // 2
    mass = jnp.concatenate([far_stats[index] for index in range(stat_half)], axis=1)
    seen = jnp.concatenate([far_stats[stat_half + index] for index in range(stat_half)], axis=1)
    scores = dot_nt(kv[0], far_qd[0]) * scale
    grads = dot_nt(kv[1], far_qd[1])
    top = jnp.maximum(mass, jnp.max(scores, axis=0, keepdims=True))
    probs = jnp.exp(scores - top)
    rest = jnp.exp(mass - top)
    inverse_total = 1.0 / (rest + jnp.sum(probs, axis=0, keepdims=True))
    probs = probs * inverse_total
    delta = seen * rest * inverse_total + jnp.sum(probs * grads, axis=0, keepdims=True)
    low = probs.astype(jnp.bfloat16)
    grad_scores = (probs * (grads - delta) * scale).astype(jnp.bfloat16)
    grad_key += dot_nn(grad_scores, far_qd[0])
    grad_value += dot_nn(low, far_qd[1])
    dk_ref[...] = grad_key.astype(jnp.bfloat16)
    dv_ref[...] = grad_value.astype(jnp.bfloat16)

    for stream, held in ((0, held_kv), (1, held_qd), (4, held_kv), (5, held_qd)):
        await_bytes(held.at[pl.ds(0, others)], send_sem.at[stream])

    @pl.when(me % stride == 0)
    def _():
        await_bytes(far_stats.at[pl.ds(0, stat_rows - 1)], send_sem.at[6])
        await_bytes(held_stats.at[pl.ds(0, others)], send_sem.at[8])

    @pl.when(me % stride != 0)
    def _():
        await_bytes(far_stats, send_sem.at[6])

    @pl.when(me < others)
    def _():
        shift_kv.wait_send()


    @pl.when(crosses)
    def _():
        await_bytes(next_qd.at[:, pl.ds(0, span // 2), :], send_sem.at[3])

    @pl.when((place > 0) & (place != half))
    def _():
        shift_qd.wait_send()

    for index in range(rows):
        meant, copy = forward(index)

        @pl.when(meant)
        def _():
            copy.wait_send()
    @pl.when(me > 0)
    def _():
        tell_prev.wait_send()


def write_kernel(*refs):
    results, places, sem = refs[:4], refs[4:8], refs[8]
    copies = [
        pltpu.make_async_copy(result, place, sem.at[index])
        for index, (result, place) in enumerate(zip(results, places))
    ]
    for copy in copies:
        copy.start()
    for copy in copies:
        copy.wait()


def body(queries, keys, values, grad_out, block_perm):
    span, width = queries.shape
    count = lax.axis_size(AXIS)
    piece = span // count
    stat_rows = 2 * span // 128
    pair = pltpu.VMEM((2, span, width), jnp.bfloat16)
    pieces = pltpu.VMEM((count, 2, piece, width), jnp.bfloat16)
    in_place = pl.BlockSpec(memory_space=pltpu.HBM)
    in_vmem = pl.BlockSpec(memory_space=pltpu.VMEM)
    result = jax.ShapeDtypeStruct((span, width), jnp.bfloat16)

    def run(*refs):
        kernel(count, *refs)

    results = pl.pallas_call(
        run,
        out_shape=(pltpu.VMEM((span, width), jnp.bfloat16),) * 4,
        in_specs=[in_place] * 5,
        out_specs=(in_vmem,) * 4,
        scratch_shapes=[
            pltpu.SMEM((1, count), jnp.int32),
            pltpu.SMEM((count,), jnp.int32),
            pair, pair, pieces, pieces, pieces, pieces, pair, pair, pair, pair,
            pltpu.VMEM((2, span), jnp.float32),
            pltpu.VMEM((2, span), jnp.float32),
            pltpu.VMEM((stat_rows, 1, 128), jnp.float32),
            pltpu.VMEM((count, 1, 128), jnp.float32),
            pltpu.VMEM((count, 1, 128), jnp.float32),
            pltpu.VMEM((stat_rows, 1, 128), jnp.float32),
            pltpu.SemaphoreType.DMA((5,)),
            pltpu.SemaphoreType.DMA((10,)),
            pltpu.SemaphoreType.DMA((9,)),
            pltpu.SemaphoreType.REGULAR((ALONG_Z,)),
            pltpu.SemaphoreType.REGULAR((ALONG_Z,)),
        ],
        compiler_params=pltpu.CompilerParams(
            collective_id=0, has_side_effects=True, vmem_limit_bytes=66400000
        ),
    )(block_perm, queries, keys, values, grad_out)
    return pl.pallas_call(
        write_kernel,
        out_shape=(result,) * 4,
        in_specs=[in_vmem] * 4,
        out_specs=(in_place,) * 4,
        scratch_shapes=[pltpu.SemaphoreType.DMA((4,))],
    )(*(pltpu.with_memory_space_constraint(result, pltpu.VMEM) for result in results))


def solution(mesh):
    placed = (
        P("seq", "head"),
        P("seq", "head"),
        P("seq", "head"),
        P("seq", "head"),
        P("head", None),
    )
    return jax.shard_map(
        body,
        mesh=mesh,
        in_specs=placed,
        out_specs=(P("seq", "head"), P("seq", "head"), P("seq", "head"), P("seq", "head")),
        check_vma=False,
    )
```

```python
import jax
import jax.numpy as jnp
from jax import lax
from jax.experimental import pallas as pl
from jax.experimental.pallas import tpu as pltpu
from jax.sharding import PartitionSpec as P

MESH = pl.DeviceIdType.MESH
AXIS = "seq"
ALONG_Z = 8
QD_EARLY = 24
QD_FIRST = 16


def dot_nt(left, right):
    return lax.dot_general(left, right, (((1,), (1,)), ((), ())), preferred_element_type=jnp.float32)


def dot_tn(left, right):
    return lax.dot_general(left, right, (((0,), (0,)), ((), ())), preferred_element_type=jnp.float32)


def dot_nn(left, right):
    return jnp.dot(left, right, preferred_element_type=jnp.float32)


def target(step, me, count):
    ring = step // (count // ALONG_Z)
    turn = (step + 1) % (count // ALONG_Z)
    along = (ALONG_Z // 2 + (1 - 2 * (ring % 2)) * ((ring + 1) // 2)) % ALONG_Z
    place = (me % ALONG_Z + along) % ALONG_Z
    row = (me // ALONG_Z + turn) % (count // ALONG_Z)
    return row * ALONG_Z + place


def outward(step, me, count):
    ring = step // (count // ALONG_Z)
    turn = step % (count // ALONG_Z)
    place = (ring % 2) * (ALONG_Z - 1) + (1 - 2 * (ring % 2)) * (ring // 2)
    return turn * ALONG_Z + place


def rows_of(index, size):
    return pl.ds(pl.multiple_of(index * size, size), size)


def await_bytes(ref, sem):
    pltpu.make_async_copy(ref, ref, sem).wait()


def kernel(
    count, perm_hbm, q_hbm, k_hbm, v_hbm, g_hbm, o_ref, dq_ref, dk_ref, dv_ref,
    perm_ref, inv, kv, qd, held_kv, held_qd, sorted_kv, sorted_qd, far_kv, far_qd, prev_kv, next_qd,
    full_stats, next_stats, part_stats, held_stats, sorted_stats, far_stats,
    in_sem, send_sem, recv_sem, up_sem, down_sem,
):
    me = lax.axis_index(AXIS)
    span, width = q_hbm.shape
    piece = span // count
    scale = width ** (-0.5)
    others = count - 1
    rows = count // ALONG_Z
    place = me % ALONG_Z
    row = me // ALONG_Z
    last = ALONG_Z - 1
    half = ALONG_Z // 2
    lanes = 128
    stat_rows = 2 * span // lanes
    stride = count // stat_rows

    def signal(sem, to):
        pl.semaphore_signal(sem, inc=1, device_id={AXIS: to}, device_id_type=MESH)

    def remote(source, landing, to, stream):
        return pltpu.make_async_remote_copy(
            src_ref=source,
            dst_ref=landing,
            send_sem=send_sem.at[stream],
            recv_sem=recv_sem.at[stream],
            device_id={AXIS: to},
            device_id_type=MESH,
        )

    barrier = pltpu.get_barrier_semaphore()
    for turn in range(1, rows):
        signal(barrier, (row + turn) % rows * ALONG_Z + place)

    @pl.when(place > 0)
    def _():
        signal(barrier, me - 1)

    @pl.when(place < last)
    def _():
        signal(barrier, me + 1)

    loads = [
        pltpu.make_async_copy(k_hbm, kv.at[0], in_sem.at[0]),
        pltpu.make_async_copy(v_hbm, kv.at[1], in_sem.at[1]),
        pltpu.make_async_copy(q_hbm, qd.at[0], in_sem.at[2]),
        pltpu.make_async_copy(g_hbm, qd.at[1], in_sem.at[3]),
        pltpu.make_async_copy(perm_hbm, perm_ref, in_sem.at[4]),
    ]
    for load in loads:
        load.start()

    greeted = rows - 1 + jnp.where(place > 0, 1, 0) + jnp.where(place < last, 1, 0)
    pl.semaphore_wait(barrier, greeted)

    @pl.when(place > 0)
    def _():
        signal(down_sem.at[0], me - 1)

    @pl.when(place < last)
    def _():
        signal(up_sem.at[0], me + 1)

    shift_kv = remote(kv, prev_kv, (me + 1) % count, 2)
    shift_qd = remote(qd, next_qd, (me + others) % count, 3)
    for load in loads[:2]:
        load.wait()

    @pl.when(place < last)
    def _():
        shift_kv.start()

    def to_piece(source, held, to, stream):
        remote(source.at[:, rows_of(to, piece), :], held.at[me], to, stream).start()

    def to_column(there):
        for turn in range(rows):
            to_piece(kv, held_kv, (row + turn) % rows * ALONG_Z + there, 0)

    for turn in range(1, rows):
        to_piece(kv, held_kv, (row + turn) % rows * ALONG_Z + place, 0)

    def below(step, carry):
        pl.semaphore_wait(up_sem.at[step], 1)

        @pl.when(place < last)
        def _():
            signal(up_sem.at[step + 1], me + 1)

        to_column(place - 1 - step)
        return carry

    lax.fori_loop(0, place, below, 0)

    def above(step, carry):
        pl.semaphore_wait(down_sem.at[step], 1)

        @pl.when(place > 0)
        def _():
            signal(down_sem.at[step + 1], me - 1)

        to_column(place + 1 + step)
        return carry

    lax.fori_loop(0, last - place, above, 0)

    @pl.when((place == last) & (me < others))
    def _():
        shift_kv.start()

    for load in loads[2:]:
        load.wait()

    own_side = place // half * half

    def near_rows(index):
        start = (index * ALONG_Z + own_side) * piece
        return pl.ds(pl.multiple_of(start, half * piece), half * piece)

    crosses = (place == half) | ((place == 0) & (me > 0))

    def shift_part(index):
        part = (slice(None), near_rows(index), slice(None))
        return remote(qd.at[part], next_qd.at[part], (me + others) % count, 3)

    def all_qd(step, carry):
        to_piece(qd, held_qd, target(step, me, count), 1)
        return carry

    @pl.when(place == 0)
    def _():
        lax.fori_loop(0, QD_FIRST, all_qd, 0)

    def invert(block, carry):
        found = jnp.int32(0)
        for query in range(count):
            found = jnp.where(perm_ref[0, query] == block, query, found)
        inv[block] = found
        return carry

    lax.fori_loop(0, count, invert, 0)
    held_kv[me] = kv[:, rows_of(me, piece), :]
    held_qd[me] = qd[:, rows_of(me, piece), :]

    @pl.when(me == 0)
    def _():
        prev_kv[...] = jnp.zeros_like(prev_kv)

    @pl.when(me == others)
    def _():
        next_qd[...] = jnp.zeros_like(next_qd)
        next_stats[...] = jnp.zeros_like(next_stats)

    def arrange(held, arranged, index_of):
        def reorder(block, carry):
            arranged[block] = held[index_of(block)]
            return carry

        lax.fori_loop(0, count, reorder, 0)

    def deliver(arranged, landing, stream, first, end):
        def issue(step, carry):
            to = outward(step, me, count)

            @pl.when(to != me)
            def _():
                remote(arranged.at[to], landing.at[:, rows_of(me, piece), :], to, stream).start()

            return carry

        lax.fori_loop(first, end, issue, 0)

    query_rows = qd[0]
    grad_rows = qd[1]
    own_scores = dot_nt(kv[0], query_rows) * scale
    own_grads = dot_nt(kv[1], grad_rows)

    @pl.when(me > 0)
    def _():
        shift_kv.wait_recv()

    prev_scores = jnp.where(me > 0, dot_nt(prev_kv[0], query_rows) * scale, -1e30)
    prev_grads = dot_nt(prev_kv[1], grad_rows)
    near_top = jnp.max(jnp.maximum(own_scores, prev_scores), axis=0, keepdims=True)
    own_probs = jnp.exp(own_scores - near_top)
    prev_probs = jnp.exp(prev_scores - near_top)
    near_total = jnp.sum(own_probs + prev_probs, axis=0, keepdims=True)
    near_mass = near_top + jnp.log(near_total)
    near_delta = (
        jnp.sum(own_probs * own_grads + prev_probs * prev_grads, axis=0, keepdims=True) / near_total
    )
    for index in range(stat_rows):
        part = near_mass if index < stat_rows // 2 else near_delta
        start = index % (stat_rows // 2) * lanes
        part_stats[index] = part[:, start : start + lanes]

    for index in range(stat_rows):

        @pl.when(me != index * stride)
        def _():
            remote(part_stats.at[index], held_stats.at[me], index * stride, 6).start()

        @pl.when(me == index * stride)
        def _():
            held_stats[me] = part_stats[index]

    lax.fori_loop(jnp.where(place == 0, QD_FIRST, 0), others, all_qd, 0)

    await_bytes(held_kv.at[pl.ds(0, others)], recv_sem.at[0])
    arrange(held_kv, sorted_kv, lambda block: perm_ref[0, block])
    deliver(sorted_kv, far_kv, 4, 0, count)
    far_kv[:, rows_of(me, piece), :] = sorted_kv[me]

    @pl.when(crosses)
    def _():
        for index in range(rows):
            shift_part(index).start()

    @pl.when((place > 0) & (place != half))
    def _():
        shift_qd.start()
    await_bytes(held_qd.at[pl.ds(0, others)], recv_sem.at[1])
    arrange(held_qd, sorted_qd, lambda block: inv[block])
    @pl.when(me % stride == 0)
    def _():
        await_bytes(held_stats.at[pl.ds(0, others)], recv_sem.at[6])
        arrange(held_stats, sorted_stats, lambda block: inv[block])

        def issue(step, carry):
            to = target(step, me, count)
            remote(sorted_stats.at[to], far_stats.at[me // stride], to, 8).start()
            return carry

        lax.fori_loop(0, others, issue, 0)
        far_stats[me // stride] = sorted_stats[me]

    def forward(index):
        there = index * ALONG_Z + jnp.where(place < half, half - 1, last)
        origin = there + 1
        part = (slice(None), rows_of(me, piece), slice(None))
        meant = (origin < count) & (there != me)
        return meant, pltpu.make_async_remote_copy(
            src_ref=held_qd.at[origin % count],
            dst_ref=next_qd.at[part],
            send_sem=send_sem.at[9],
            recv_sem=recv_sem.at[3],
            device_id={AXIS: there},
            device_id_type=MESH,
        )

    for index in range(rows):
        meant, copy = forward(index)

        @pl.when(meant)
        def _():
            copy.start()

    @pl.when(((place == half - 1) | (place == last)) & (me < others))
    def _():
        next_qd[:, rows_of(me, piece), :] = held_qd[(me + 1) % count]

    deliver(sorted_qd, far_qd, 5, 0, QD_EARLY)
    far_qd[:, rows_of(me, piece), :] = sorted_qd[me]

    await_bytes(held_kv.at[pl.ds(0, others)], recv_sem.at[4])

    far_scores = dot_nt(far_kv[0], query_rows) * scale
    far_grads = dot_nt(far_kv[1], grad_rows)
    far_top = jnp.max(far_scores, axis=0, keepdims=True)
    top = jnp.maximum(near_top, far_top)
    far_probs = jnp.exp(far_scores - top)
    near_weight = jnp.exp(near_top - top)
    total = near_total * near_weight + jnp.sum(far_probs, axis=0, keepdims=True)
    inverse_total = 1.0 / total
    near_weight = near_weight * inverse_total
    far_probs = far_probs * inverse_total
    delta = near_delta * near_total * near_weight + jnp.sum(
        far_probs * far_grads, axis=0, keepdims=True
    )
    full_stats[...] = jnp.concatenate([top + jnp.log(total), delta], axis=0)
    deliver(sorted_qd, far_qd, 5, QD_EARLY, count)
    tell_prev = remote(full_stats, next_stats, (me + others) % count, 7)

    @pl.when(me > 0)
    def _():
        tell_prev.start()

    attended = jnp.zeros((span, width), jnp.float32)
    grad_query = jnp.zeros((span, width), jnp.float32)
    for probs, grads, pair, own in (
        (own_probs * near_weight, own_grads, kv, True),
        (prev_probs * near_weight, prev_grads, prev_kv, False),
        (far_probs, far_grads, far_kv, False),
    ):
        low = probs.astype(jnp.bfloat16)
        grad_scores = (probs * (grads - delta) * scale).astype(jnp.bfloat16)
        attended += dot_tn(low, pair[1])
        grad_query += dot_tn(grad_scores, pair[0])
        if own:
            grad_key = dot_nn(grad_scores, query_rows)
            grad_value = dot_nn(low, grad_rows)
    o_ref[...] = attended.astype(jnp.bfloat16)
    dq_ref[...] = grad_query.astype(jnp.bfloat16)

    gathers = ((place == half - 1) | (place == last)) & (me < others)

    @pl.when(gathers)
    def _():
        await_bytes(next_qd.at[:, pl.ds(0, span - piece), :], recv_sem.at[3])

    @pl.when((place != half - 1) & (place != last))
    def _():
        shift_qd.wait_recv()
    @pl.when(me < others)
    def _():
        tell_prev.wait_recv()

    next_scores = dot_nt(kv[0], next_qd[0]) * scale
    next_grads = dot_nt(kv[1], next_qd[1])
    probs = jnp.exp(next_scores - next_stats[0:1])
    low = probs.astype(jnp.bfloat16)
    grad_scores = (probs * (next_grads - next_stats[1:2]) * scale).astype(jnp.bfloat16)
    grad_key += dot_nn(grad_scores, next_qd[0])
    grad_value += dot_nn(low, next_qd[1])

    await_bytes(held_qd.at[pl.ds(0, others)], recv_sem.at[5])

    @pl.when(me % stride == 0)
    def _():
        await_bytes(far_stats.at[pl.ds(0, stat_rows - 1)], recv_sem.at[8])

    @pl.when(me % stride != 0)
    def _():
        await_bytes(far_stats, recv_sem.at[8])

    stat_half = stat_rows // 2
    mass = jnp.concatenate([far_stats[index] for index in range(stat_half)], axis=1)
    seen = jnp.concatenate([far_stats[stat_half + index] for index in range(stat_half)], axis=1)
    scores = dot_nt(kv[0], far_qd[0]) * scale
    grads = dot_nt(kv[1], far_qd[1])
    top = jnp.maximum(mass, jnp.max(scores, axis=0, keepdims=True))
    probs = jnp.exp(scores - top)
    rest = jnp.exp(mass - top)
    inverse_total = 1.0 / (rest + jnp.sum(probs, axis=0, keepdims=True))
    probs = probs * inverse_total
    delta = seen * rest * inverse_total + jnp.sum(probs * grads, axis=0, keepdims=True)
    low = probs.astype(jnp.bfloat16)
    grad_scores = (probs * (grads - delta) * scale).astype(jnp.bfloat16)
    grad_key += dot_nn(grad_scores, far_qd[0])
    grad_value += dot_nn(low, far_qd[1])
    dk_ref[...] = grad_key.astype(jnp.bfloat16)
    dv_ref[...] = grad_value.astype(jnp.bfloat16)

    for stream, held in ((0, held_kv), (1, held_qd), (4, held_kv), (5, held_qd)):
        await_bytes(held.at[pl.ds(0, others)], send_sem.at[stream])

    @pl.when(me % stride == 0)
    def _():
        await_bytes(far_stats.at[pl.ds(0, stat_rows - 1)], send_sem.at[6])
        await_bytes(held_stats.at[pl.ds(0, others)], send_sem.at[8])

    @pl.when(me % stride != 0)
    def _():
        await_bytes(far_stats, send_sem.at[6])

    @pl.when(me < others)
    def _():
        shift_kv.wait_send()


    @pl.when(crosses)
    def _():
        await_bytes(next_qd.at[:, pl.ds(0, span // 2), :], send_sem.at[3])

    @pl.when((place > 0) & (place != half))
    def _():
        shift_qd.wait_send()

    for index in range(rows):
        meant, copy = forward(index)

        @pl.when(meant)
        def _():
            copy.wait_send()
    @pl.when(me > 0)
    def _():
        tell_prev.wait_send()


def write_kernel(*refs):
    results, places, sem = refs[:4], refs[4:8], refs[8]
    copies = [
        pltpu.make_async_copy(result, place, sem.at[index])
        for index, (result, place) in enumerate(zip(results, places))
    ]
    for copy in copies:
        copy.start()
    for copy in copies:
        copy.wait()


def body(queries, keys, values, grad_out, block_perm):
    span, width = queries.shape
    count = lax.axis_size(AXIS)
    piece = span // count
    stat_rows = 2 * span // 128
    pair = pltpu.VMEM((2, span, width), jnp.bfloat16)
    pieces = pltpu.VMEM((count, 2, piece, width), jnp.bfloat16)
    in_place = pl.BlockSpec(memory_space=pltpu.HBM)
    in_vmem = pl.BlockSpec(memory_space=pltpu.VMEM)
    result = jax.ShapeDtypeStruct((span, width), jnp.bfloat16)

    def run(*refs):
        kernel(count, *refs)

    results = pl.pallas_call(
        run,
        out_shape=(pltpu.VMEM((span, width), jnp.bfloat16),) * 4,
        in_specs=[in_place] * 5,
        out_specs=(in_vmem,) * 4,
        scratch_shapes=[
            pltpu.SMEM((1, count), jnp.int32),
            pltpu.SMEM((count,), jnp.int32),
            pair, pair, pieces, pieces, pieces, pieces, pair, pair, pair, pair,
            pltpu.VMEM((2, span), jnp.float32),
            pltpu.VMEM((2, span), jnp.float32),
            pltpu.VMEM((stat_rows, 1, 128), jnp.float32),
            pltpu.VMEM((count, 1, 128), jnp.float32),
            pltpu.VMEM((count, 1, 128), jnp.float32),
            pltpu.VMEM((stat_rows, 1, 128), jnp.float32),
            pltpu.SemaphoreType.DMA((5,)),
            pltpu.SemaphoreType.DMA((10,)),
            pltpu.SemaphoreType.DMA((9,)),
            pltpu.SemaphoreType.REGULAR((ALONG_Z,)),
            pltpu.SemaphoreType.REGULAR((ALONG_Z,)),
        ],
        compiler_params=pltpu.CompilerParams(
            collective_id=0, has_side_effects=True, vmem_limit_bytes=66400000
        ),
    )(block_perm, queries, keys, values, grad_out)
    return pl.pallas_call(
        write_kernel,
        out_shape=(result,) * 4,
        in_specs=[in_vmem] * 4,
        out_specs=(in_place,) * 4,
        scratch_shapes=[pltpu.SemaphoreType.DMA((4,))],
    )(*(pltpu.with_memory_space_constraint(result, pltpu.VMEM) for result in results))


def solution(mesh):
    placed = (
        P("seq", "head"),
        P("seq", "head"),
        P("seq", "head"),
        P("seq", "head"),
        P("head", None),
    )
    return jax.shard_map(
        body,
        mesh=mesh,
        in_specs=placed,
        out_specs=(P("seq", "head"), P("seq", "head"), P("seq", "head"), P("seq", "head")),
        check_vma=False,
    )
```
